128 devices in a mesh: tp: 8 (over y, x_lo), lat: 16 (over x_hi, z, core).
Axes of the slice: x: 4 (x_hi: 2, x_lo: 2; x = x_hi * 2 + x_lo), y: 4, z: 4, core: 2. Of those that a mesh axis runs over, the one named last changes fastest.
Arguments:
- attn_out: bfloat16 [2048, 4096], P('lat', 'tp'), may hold values from -6 to 6
- w_out: bfloat16 [4096, 8192], P('tp'), may hold values from -0.09375 to 0.09375
- resid_in: bfloat16 [2048, 8192], P(('lat', 'tp')), may hold values from -6 to 6
- positions: int32 [256], replicated, may hold values from 0 to 2047
- w_enc: bfloat16 [8192, 131072], P(None, ('tp', 'lat')), may hold values from -0.0625 to 0.0625
- b_enc: float32 [131072], P(('tp', 'lat')), may hold values from -3 to 3
- dec_norm: float32 [131072], P(('tp', 'lat')), may hold values from 0.05 to 0.5
- b_dec: float32 [8192], replicated, may hold values from -3 to 3
Outputs:
- stream: bfloat16 [2048, 8192], P(('lat', 'tp'))
- codes: bfloat16 [256, 131072], P(None, ('tp', 'lat'))
- recon: bfloat16 [256, 8192], P(('tp', 'lat'))
- error: float32 [256], P(('tp', 'lat'))
The draws below stay inside these ranges and needn't reach their ends.
All inputs are finite; a program needn't handle non-finite values.
Results may differ from the reference program's by a relative error of at most 0.0059.
Values may be sent and summed in bfloat16 or wider, within the bound.
No kernel may reach another device: no remote copies, remote signals or barrier semaphores. Data moves between devices by JAX's collectives and lax.ppermute only.
A program may use at most 128 MiB of HBM per device.

```python
import math
import jax
import jax.numpy as jnp
from jax import lax

D = 8192
HD = 128
HEADS = 32
LATENTS = 131072
TOKENS = 2048
SEL = 256


def set_ends(values, stream_key, smallest, largest):
    longest = values.shape.index(max(values.shape))
    spots = []
    for shift in (0, 1):
        where = [jax.random.randint(jax.random.fold_in(stream_key, axis), (), 0, length) for axis, length in enumerate(values.shape)]
        where[longest] = (where[longest] + shift) % values.shape[longest]
        spots.append(tuple(where))
    return values.at[spots[0]].set(smallest).at[spots[1]].set(largest)


def levels(own_key, extent, cuts, smallest, largest):
    def one(axis_at, blocks):
        draws = jax.random.uniform(jax.random.fold_in(jax.random.fold_in(own_key, 6), axis_at), (blocks,), jnp.float32, smallest / len(cuts), largest / len(cuts))
        return jnp.repeat(jnp.exp(draws), extent[axis_at] // blocks).reshape((-1,) + (1,) * (len(extent) - axis_at - 1))

    loudness = one(*cuts[0])
    for cut in cuts[1:]:
        loudness = loudness * one(*cut)
    return loudness


def scatter_about(stream_key, dims, width, reach, pieces=(), dtype=jnp.bfloat16):
    drawn = width * jax.random.normal(stream_key, dims, jnp.float32)
    if pieces:
        drawn = drawn * levels(stream_key, dims, pieces, -0.22, 0.18)
    return jnp.clip(drawn, -reach, reach).astype(dtype)


def setup_inputs(seed: int = 0) -> dict:
    streams_of = jax.random.split(jax.random.key(seed), 9)
    attn_out = scatter_about(streams_of[0], (TOKENS, HEADS * HD), 1.0, 6.0, ((0, 16), (1, 8)))
    w_out = scatter_about(streams_of[1], (HEADS * HD, D), (HEADS * HD) ** -0.5, 0.09375, ((0, 8),))
    resid_in = scatter_about(streams_of[2], (TOKENS, D), 1.0, 6.0, ((0, 128),))
    positions = set_ends(jax.random.randint(streams_of[3], (SEL,), 0, TOKENS), jax.random.fold_in(streams_of[3], 1), 0, TOKENS - 1).astype(jnp.int32)
    w_enc = scatter_about(streams_of[4], (D, LATENTS), D ** -0.5, 0.0625, ((1, 128),))
    b_enc = scatter_about(streams_of[5], (LATENTS,), 0.5, 3.0, ((0, 128),), jnp.float32)
    dec_norm = jnp.clip(jnp.exp(math.log(0.5) - 2.3025851 * jax.random.uniform(streams_of[6], (LATENTS,), jnp.float32) ** levels(streams_of[6], (LATENTS,), ((0, 128),), -0.2, 0.2)), 0.05, 0.5)
    b_dec = scatter_about(streams_of[7], (D,), 0.5, 3.0, (), jnp.float32)
    return dict(attn_out=attn_out, w_out=w_out, resid_in=resid_in, positions=positions, w_enc=w_enc, b_enc=b_enc, dec_norm=dec_norm, b_dec=b_dec)


def reference(attn_out, w_out, resid_in, positions, w_enc, b_enc, dec_norm, b_dec):
    mixed = jnp.dot(attn_out, w_out, preferred_element_type=jnp.float32)
    stream = (resid_in.astype(jnp.float32) + mixed).astype(jnp.bfloat16)
    picked = jnp.take(stream, positions.astype(jnp.int32), axis=0)
    centered = (picked.astype(jnp.float32) - b_dec).astype(jnp.bfloat16)
    pre = jnp.dot(centered, w_enc, preferred_element_type=jnp.float32) + b_enc
    codes = (jnp.maximum(pre, 0.0) * dec_norm).astype(jnp.bfloat16)
    full = lax.dot_general(codes, w_enc, (((1,), (1,)), ((), ())), preferred_element_type=jnp.float32) + b_dec
    recon = full.astype(jnp.bfloat16)
    error = jnp.mean((full - picked.astype(jnp.float32)) ** 2, axis=1)
    return stream, codes, recon, error
```

```python
import functools

import jax
import jax.numpy as jnp
from jax import lax
from jax.experimental import pallas as pl
from jax.experimental.pallas import tpu as pltpu
from jax.sharding import Mesh, PartitionSpec as P

AXES = ("y", "xl", "xh", "z", "c")
SIZES = (4, 2, 2, 4, 2)
TP = ("y", "xl")
LAT = ("xh", "z", "c")
bf16 = jnp.bfloat16
f32 = jnp.float32


def _x(i):
    i %= 4
    return (i % 2) * 2 + i // 2


def shift(v, ax, s):
    if ax == "x":
        return lax.ppermute(v, ("xl", "xh"), [(_x(i), _x(i + s)) for i in range(4)])
    n = 4 if ax in "yz" else 2
    return lax.ppermute(v, ax, [(i, (i + s) % n) for i in range(n)])


def coord(ax):
    if ax == "x":
        return lax.axis_index("xh") * 2 + lax.axis_index("xl")
    return lax.axis_index(ax)


def take(v, i, axis=0):
    return lax.dynamic_index_in_dim(v, i, axis, keepdims=False)


def reduce_ring(v, ax):
    me = coord(ax)
    got = [shift(take(v, (me + s) % 4), ax, s) for s in (2, 1, 3)]
    total = take(v, me).astype(f32)
    for g in got:
        total = total + g.astype(f32)
    return total


def gather_ring(v, ax):
    got = {s: shift(v, ax, s) for s in (2, 1, 3)}
    return jnp.stack([v, got[1], got[2], got[3]])


VMEM_LIMIT = 56 * 1024 * 1024


def project(cols, attn, place, w_out, resid, counts, dtypes):
    starts = [sum(counts[:j]) for j in range(len(counts))]
    steps = sum(counts)
    rows, width = attn.shape[0], 512

    def kernel(cols_ref, attn_ref, place_ref, w_ref, r_ref, *outs):
        i = pl.program_id(0)
        acc = jnp.dot(attn_ref[...], w_ref[...], preferred_element_type=f32)
        acc = acc + jnp.dot(place_ref[...], r_ref[...], preferred_element_type=f32)
        for o, first, n in zip(outs, starts, counts):

            @pl.when((i >= first) & (i < first + n))
            def _():
                o[0] = acc.astype(o.dtype)

    def out_map(first, n):
        return lambda i, cols: (jnp.clip(i - first, 0, n - 1), 0, 0)

    return pl.pallas_call(
        kernel,
        grid_spec=pltpu.PrefetchScalarGridSpec(
            num_scalar_prefetch=1,
            grid=(steps,),
            in_specs=[
                pl.BlockSpec(attn.shape, lambda i, cols: (0, 0)),
                pl.BlockSpec(place.shape, lambda i, cols: (0, 0)),
                pl.BlockSpec((w_out.shape[0], width), lambda i, cols: (0, cols[i])),
                pl.BlockSpec((resid.shape[0], width), lambda i, cols: (0, cols[i])),
            ],
            out_specs=[pl.BlockSpec((1, rows, width), out_map(a, n)) for a, n in zip(starts, counts)],
        ),
        out_shape=[jax.ShapeDtypeStruct((n, rows, width), d) for n, d in zip(counts, dtypes)],
        name="project",
    )(cols, attn, place, w_out, resid)


def encode(order, own, oth, w_enc, b_dec, acc, b_enc, dec_norm):
    n, half, width = own.shape
    lat = w_enc.shape[1]
    last = b_enc is not None

    def kernel(order_ref, own_ref, oth_ref, w_ref, bd_ref, *rest):
        i = pl.program_id(0)
        rest = list(rest)
        acc_in = rest.pop(0) if acc is not None else None
        if last:
            be_ref, dn_ref, out_ref, acc_ref = rest
        else:
            (acc_ref,) = rest
        bd = bd_ref[0]
        lhs = jnp.concatenate([own_ref[0], oth_ref[0]], axis=0)
        lhs = (lhs.astype(f32) - bd).astype(bf16)
        term = jnp.dot(lhs, w_ref[...], preferred_element_type=f32)

        @pl.when(i == 0)
        def _():
            acc_ref[...] = term if acc_in is None else acc_in[...] + term

        @pl.when(i > 0)
        def _():
            acc_ref[...] += term

        if last:

            @pl.when(i == n - 1)
            def _():
                pre = acc_ref[...] + be_ref[...]
                out_ref[...] = (jnp.maximum(pre, 0.0) * dn_ref[...]).astype(bf16)

    whole = lambda shape: pl.BlockSpec(shape, lambda i, order: (0,) * len(shape))
    in_specs = [
        pl.BlockSpec((1, half, width), lambda i, order: (i, 0, 0)),
        pl.BlockSpec((1, half, width), lambda i, order: (i, 0, 0)),
        pl.BlockSpec((width, lat), lambda i, order: (order[i], 0)),
        pl.BlockSpec((1, 1, width), lambda i, order: (order[i], 0, 0)),
    ]
    args = [own, oth, w_enc, b_dec.reshape(-1, 1, width)]
    if acc is not None:
        in_specs.append(whole((2 * half, lat)))
        args.append(acc)
    if last:
        in_specs += [whole((1, lat)), whole((1, lat))]
        args += [b_enc[None], dec_norm[None]]
    return pl.pallas_call(
        kernel,
        grid_spec=pltpu.PrefetchScalarGridSpec(
            num_scalar_prefetch=1,
            grid=(n,),
            in_specs=in_specs,
            out_specs=whole((2 * half, lat)),
            scratch_shapes=[pltpu.VMEM((2 * half, lat), f32)] if last else [],
        ),
        out_shape=jax.ShapeDtypeStruct((2 * half, lat), bf16 if last else f32),
        name="encode",
    )(order, *args)


def decode(codes, w_enc, first, n):
    rows, lat = codes.shape
    half, width = rows // 2, 512

    def kernel(codes_ref, w_ref, own_ref, oth_ref):
        r = lax.dot_general(codes_ref[...], w_ref[...], (((1,), (1,)), ((), ())), preferred_element_type=f32)
        own_ref[...] = r[:half].astype(own_ref.dtype)
        oth_ref[...] = r[half:].astype(oth_ref.dtype)

    return pl.pallas_call(
        kernel,
        grid=(n,),
        in_specs=[
            pl.BlockSpec((rows, lat), lambda i: (0, 0)),
            pl.BlockSpec((width, lat), lambda i: (i + first, 0)),
        ],
        out_specs=[pl.BlockSpec((half, width), lambda i: (0, i))] * 2,
        out_shape=[jax.ShapeDtypeStruct((half, n * width), f32), jax.ShapeDtypeStruct((half, n * width), bf16)],
        name="decode",
    )(codes, w_enc)


def shards(attn_out, w_out, resid_in, positions, w_enc, b_enc, dec_norm, b_dec):
    y, xl, xh, z, c = (lax.axis_index(a) for a in AXES)
    x = coord("x")
    t = y * 2 + xl
    lat = xh * 8 + z * 2 + c
    own_rows = resid_in.shape[0]
    rows = attn_out.shape[0]
    d_model = w_out.shape[1]

    place = (lax.broadcasted_iota(jnp.int32, (rows, own_rows), 0) == t * own_rows + lax.broadcasted_iota(jnp.int32, (rows, own_rows), 1)).astype(bf16)

    def block(dy, dx, h):
        return ((y + dy) % 4) * 4 + (xl ^ dx) * 2 + h

    sends = [block(dy, 1, 0) for dy in range(4)] + [block(dy, dx, 1) for dy in (2, 1, 3) for dx in (0, 1)]
    keeps = [block(dy, 0, 0) for dy in range(4)] + [block(0, dx, 1) for dx in (0, 1)]
    a_send, b2, b1, b3 = project(jnp.stack(sends), attn_out, place, w_out, resid_in, (4, 2, 2, 2), (bf16,) * 4)
    a_got = shift(a_send, "xl", 1)
    b_got = [shift(b2, "y", 2), shift(b1, "y", 1), shift(b3, "y", 3)]
    a_keep, b_keep = project(jnp.stack(keeps), attn_out, place, w_out, resid_in, (4, 2), (f32, f32))
    a = a_keep + a_got.astype(f32)
    a_bf = a.astype(bf16)
    a_more = [shift(a_bf[s], "y", s) for s in (2, 1, 3)]
    b = b_keep
    for g in b_got:
        b = b + g.astype(f32)
    b_more = shift(b[1].astype(bf16), "xl", 1)
    a_sum = a[0]
    for g in a_more:
        a_sum = a_sum + g.astype(f32)
    b_sum = b[0] + b_more.astype(f32)
    stream = jnp.concatenate([a_sum, b_sum], axis=1).astype(bf16)

    s4 = stream.reshape(4, 2, own_rows, 1024)
    s_got = shift(take(s4, 1 - xl, 1), "xl", 1)
    s_own = take(s4, xl, 1)
    s_two = jnp.where(xl == 0, jnp.concatenate([s_own, s_got], -1), jnp.concatenate([s_got, s_own], -1))
    out = jnp.zeros((own_rows, d_model), bf16)
    out = lax.dynamic_update_slice(out, take(s_two, y), (0, y * 2048))
    for s in (2, 1, 3):
        out = lax.dynamic_update_slice(out, shift(take(s_two, (y + s) % 4), "y", s), (0, ((y - s) % 4) * 2048))
    stream_out = out

    def by_core(v):
        return v.reshape(4, 2, 2, 4, 2, 2).transpose(4, 0, 2, 1, 3, 5).reshape(2, 128)

    pos2 = by_core(positions)
    ids = lat * rows + lax.iota(jnp.int32, rows)

    def pick(p):
        hot = (p[:, None] == ids[None, :]).astype(bf16)
        return jnp.dot(hot, stream, preferred_element_type=f32).astype(bf16)

    v = shift(pick(take(pos2, 1 - c)), "c", 1) + pick(take(pos2, c))
    v2 = v.reshape(128, 2, 512)
    v = shift(take(v2, 1 - xh, 1), "xh", 1) + take(v2, xh, 1)
    got = [shift(v, "z", s) for s in (2, 1, 3)]
    v = v + got[0] + got[1] + got[2]

    a = gather_ring(v[:, :256], "x")
    b = gather_ring(v[:, 256:], "y")
    a = gather_ring(a, "y").reshape(16, 128, 256)
    b = gather_ring(b, "x").reshape(16, 128, 256)
    a_oth = shift(a, "c", 1)
    b_oth = shift(b, "c", 1)

    def chunk(sy, sx, h):
        xx = (x - sx) % 4
        return ((y - sy) % 4) * 8 + (xx % 2) * 4 + (xx // 2) * 2 + h

    a_order = jnp.stack([chunk(sy, sx, 0) for sy in range(4) for sx in range(4)])
    b_order = jnp.stack([chunk(sy, sx, 1) for sx in range(4) for sy in range(4)])

    acc = encode(a_order, a, a_oth, w_enc, b_dec, None, None, None)
    codes = encode(b_order, b, b_oth, w_enc, b_dec, acc, b_enc, dec_norm)
    own_a, oth_a = decode(codes, w_enc, 0, 8)
    got_a = shift(oth_a, "c", 1)
    own_b, oth_b = decode(codes, w_enc, 8, 8)
    got_b = shift(oth_b, "c", 1)

    idx2 = by_core(lax.iota(jnp.int32, 256))
    where = jnp.concatenate([take(idx2, c), take(idx2, 1 - c)])
    back = (lax.iota(jnp.int32, 256)[:, None] == where[None, :]).astype(bf16)
    codes_out = jnp.dot(back, codes, preferred_element_type=f32).astype(bf16)

    h_a = (own_a + got_a.astype(f32)).astype(bf16).reshape(4, 4, 8, 4096)
    h_b = (own_b + got_b.astype(f32)).astype(bf16).reshape(4, 4, 8, 4096)
    r_a = reduce_ring(h_a, "y").astype(bf16)
    r_b = reduce_ring(jnp.moveaxis(h_b, 1, 0), "x").astype(bf16)
    r_a = reduce_ring(r_a, "x")
    r_b = reduce_ring(r_b, "y")
    r = jnp.concatenate([r_a, r_b], axis=1).astype(bf16).reshape(4, 2, 8192)
    full = reduce_ring(r, "z") + b_dec

    first = (y * 4 + x) * 8 + z * 2
    mine_a = lax.dynamic_slice_in_dim(a, first, 2, 1)
    mine_b = lax.dynamic_slice_in_dim(b, first, 2, 1)
    mine = jnp.concatenate([mine_a, mine_b])
    places = jnp.concatenate([a_order, b_order])
    unsort = (lax.iota(jnp.int32, 32)[:, None] == places[None, :]).astype(bf16)
    mine = jnp.dot(unsort, mine.reshape(32, 512), preferred_element_type=f32)
    mine = mine.reshape(32, 2, 256).transpose(1, 0, 2).reshape(2, 8192)
    error = jnp.mean((full - mine) ** 2, axis=1)
    return stream_out, codes_out, full.astype(bf16), error


def solution(mesh):
    fine = Mesh(mesh.devices.reshape(SIZES), AXES)
    return jax.shard_map(
        shards,
        mesh=fine,
        in_specs=(
            P(LAT, TP),
            P(TP, None),
            P(LAT + TP, None),
            P(),
            P(None, TP + LAT),
            P(TP + LAT),
            P(TP + LAT),
            P(),
        ),
        out_specs=(
            P(LAT + TP, None),
            P(None, TP + LAT),
            P(TP + LAT, None),
            P(TP + LAT),
        ),
        check_vma=False,
    )
```

```python
import jax
import jax.numpy as jnp
from jax import lax
from jax.experimental import pallas as pl
from jax.experimental.pallas import tpu as pltpu
from jax.sharding import Mesh, PartitionSpec as P

AXES = ("y", "xl", "xh", "z", "c")
SIZES = (4, 2, 2, 4, 2)
TP = ("y", "xl")
LAT = ("xh", "z", "c")
bf16 = jnp.bfloat16
f32 = jnp.float32


def _x(i):
    i %= 4
    return (i % 2) * 2 + i // 2


def shift(v, ax, s):
    if ax == "x":
        return lax.ppermute(v, ("xl", "xh"), [(_x(i), _x(i + s)) for i in range(4)])
    n = 4 if ax in "yz" else 2
    return lax.ppermute(v, ax, [(i, (i + s) % n) for i in range(n)])


def coord(ax):
    if ax == "x":
        return lax.axis_index("xh") * 2 + lax.axis_index("xl")
    return lax.axis_index(ax)


def take(v, i, axis=0):
    return lax.dynamic_index_in_dim(v, i, axis, keepdims=False)


def reduce_ring(v, ax):
    me = coord(ax)
    got = [shift(take(v, (me + s) % 4), ax, s) for s in (2, 1, 3)]
    total = take(v, me).astype(f32)
    for g in got:
        total = total + g.astype(f32)
    return total


def gather_ring(v, ax):
    got = {s: shift(v, ax, s) for s in (2, 1, 3)}
    return jnp.stack([v, got[1], got[2], got[3]])


def swap(v, ax, bit):
    if ax == "x":
        return lax.ppermute(v, ("xl", "xh"), [(_x(i), _x(i ^ bit)) for i in range(4)])
    return lax.ppermute(v, ax, [(i, i ^ bit) for i in range(4)])


def gather_double(v, ax):
    two = jnp.stack([v, swap(v, ax, 1)])
    return jnp.concatenate([two, swap(two, ax, 2)])


def reduce_double(v, ax):
    me = coord(ax)
    v = v.reshape((2, 2) + v.shape[1:])
    for bit, axis in ((1, 1), (2, 0)):
        mine = (me // bit) % 2
        v = take(v, mine, axis) + swap(take(v, 1 - mine, axis).astype(bf16), ax, bit).astype(f32)
    return v


VM = pl.BlockSpec(memory_space=pltpu.VMEM)
SM = pl.BlockSpec(memory_space=pltpu.SMEM)
HB = pl.BlockSpec(memory_space=pl.ANY)


def limit(mib):
    return pltpu.CompilerParams(vmem_limit_bytes=mib * 1024 * 1024)


def project(cols, attn, place, w_out, resid, counts, dtypes):
    rows, width, steps = attn.shape[0], 512, sum(counts)

    def kernel(cols_ref, attn_ref, place_ref, w_ref, r_ref, *rest):
        outs, buf, sems = rest[:-2], rest[-2], rest[-1]

        def span(i):
            return pl.ds(pl.multiple_of(cols_ref[i] * width, width), width)

        copies = [pltpu.make_async_copy(w_ref.at[:, span(i)], buf.at[i], sems.at[i]) for i in range(steps)]
        for copy in copies:
            copy.start()
        slots = [(o, j) for o, n in zip(outs, counts) for j in range(n)]
        for i, (o, j) in enumerate(slots):
            copies[i].wait()
            acc = jnp.dot(attn_ref[...], buf[i], preferred_element_type=f32)
            acc = acc + jnp.dot(place_ref[...], r_ref[:, span(i)], preferred_element_type=f32)
            o[j] = acc.astype(o.dtype)

    return pl.pallas_call(
        kernel,
        in_specs=[SM, VM, VM, HB, VM],
        out_specs=[VM] * len(counts),
        out_shape=[jax.ShapeDtypeStruct((n, rows, width), d) for n, d in zip(counts, dtypes)],
        scratch_shapes=[pltpu.VMEM((steps, w_out.shape[0], width), bf16), pltpu.SemaphoreType.DMA((steps,))],
        compiler_params=limit(24),
        name="project",
    )(cols, attn, place, w_out, resid)


def encode(index, units, own, oth, w_enc, b_dec, acc, b_enc, dec_norm):
    _, _, half, width = own.shape
    lat = w_enc.shape[1]
    last = b_enc is not None

    def kernel(index_ref, units_ref, own_ref, oth_ref, w_ref, bd_ref, *rest):
        out_ref = rest[-1]
        total = rest[0][...] if acc is not None else None
        for i in range(4):
            for k in range(4):
                at = index_ref[i * 4 + k]
                unit = units_ref[i * 4 + k]
                lhs = jnp.concatenate([own_ref[i, at], oth_ref[i, at]], axis=0)
                lhs = (lhs.astype(f32) - bd_ref[unit]).astype(bf16)
                rows = pl.ds(pl.multiple_of(unit * width, width), width)
                term = jnp.dot(lhs, w_ref[rows], preferred_element_type=f32)
                total = term if total is None else total + term
        if last:
            pre = total + rest[-3][...]
            out_ref[...] = (jnp.maximum(pre, 0.0) * rest[-2][...]).astype(bf16)
        else:
            out_ref[...] = total

    args = [index, units, own, oth, w_enc, b_dec.reshape(-1, 1, width)]
    if acc is not None:
        args.append(acc)
    if last:
        args += [b_enc[None], dec_norm[None]]
    return pl.pallas_call(
        kernel,
        in_specs=[SM, SM] + [VM] * (len(args) - 2),
        out_specs=VM,
        out_shape=jax.ShapeDtypeStruct((2 * half, lat), bf16 if last else f32),
        compiler_params=limit(16),
        name="encode",
    )(*args)


def decode(codes, w_enc, first, n):
    rows = codes.shape[0]
    half, width = rows // 2, 512

    def kernel(codes_ref, w_ref, own_ref, oth_ref):
        for i in range(n // width):
            w = w_ref[first + i * width : first + (i + 1) * width]
            r = lax.dot_general(codes_ref[...], w, (((1,), (1,)), ((), ())), preferred_element_type=f32)
            own_ref[:, i * width : (i + 1) * width] = r[:half]
            oth_ref[:, i * width : (i + 1) * width] = r[half:].astype(bf16)

    return pl.pallas_call(
        kernel,
        in_specs=[VM, VM],
        out_specs=[VM, VM],
        out_shape=[jax.ShapeDtypeStruct((half, n), f32), jax.ShapeDtypeStruct((half, n), bf16)],
        compiler_params=limit(16),
        name="decode",
    )(codes, w_enc)


def shards(attn_out, w_out, resid_in, positions, w_enc, b_enc, dec_norm, b_dec):
    y, xl, xh, z, c = (lax.axis_index(a) for a in AXES)
    x = coord("x")
    t = y * 2 + xl
    lat = xh * 8 + z * 2 + c
    own_rows = resid_in.shape[0]
    rows = attn_out.shape[0]

    place = (lax.broadcasted_iota(jnp.int32, (rows, own_rows), 0) == t * own_rows + lax.broadcasted_iota(jnp.int32, (rows, own_rows), 1)).astype(bf16)

    def block(dy, dx, h):
        yy, xx = (y + dy) % 4, xl ^ dx
        return 8 + xx * 4 + yy if h else yy * 2 + xx

    cols = [block(dy, 1, 0) for dy in range(4)] + [block(dy, dx, 1) for dy in (2, 1, 3) for dx in (0, 1)]
    cols += [block(dy, 0, 0) for dy in range(4)] + [block(0, dx, 1) for dx in (0, 1)]
    a_send, b2, b1, b3, a_keep, b_keep = project(
        jnp.stack(cols), attn_out, place, w_out, resid_in, (4, 2, 2, 2, 4, 2), (bf16,) * 4 + (f32,) * 2
    )
    w_enc, a_send = lax.optimization_barrier((w_enc, a_send))
    w_near = pltpu.with_memory_space_constraint(w_enc, pltpu.VMEM)
    a_got = shift(a_send, "xl", 1)
    b_got = [shift(b2, "y", 2), shift(b1, "y", 1), shift(b3, "y", 3)]
    a = a_keep + a_got.astype(f32)
    a_bf = a.astype(bf16)
    a_more = [shift(a_bf[s], "y", s) for s in (2, 1, 3)]
    b = b_keep
    for g in b_got:
        b = b + g.astype(f32)
    b_more = shift(b[1].astype(bf16), "xl", 1)
    a_sum = a[0]
    for g in a_more:
        a_sum = a_sum + g.astype(f32)
    b_sum = b[0] + b_more.astype(f32)
    stream = jnp.concatenate([a_sum, b_sum], axis=1).astype(bf16)

    def by_core(v):
        return v.reshape(4, 2, 2, 4, 2, 2).transpose(4, 0, 2, 1, 3, 5).reshape(2, 128)

    pos2 = by_core(positions)
    ids = lat * rows + lax.iota(jnp.int32, rows)

    def pick(p):
        hot = (p[:, None] == ids[None, :]).astype(bf16)
        return jnp.dot(hot, stream, preferred_element_type=f32).astype(bf16)

    v = shift(pick(take(pos2, 1 - c)), "c", 1) + pick(take(pos2, c))
    v = v.reshape(128, 2, 2, 256)
    v = shift(take(v, 1 - xh, 2), "xh", 1) + take(v, xh, 2)
    got = [shift(v, "z", s) for s in (2, 1, 3)]
    v = v + got[0] + got[1] + got[2]

    a = gather_double(v[:, 0], "x")
    b = gather_double(v[:, 1], "y")
    a = gather_ring(a, "y")
    b = gather_ring(b, "x")
    a_oth = shift(a, "c", 1)
    b_oth = shift(b, "c", 1)

    def unit(yy, xx, h):
        return 16 + (xx % 2) * 8 + yy * 2 + xx // 2 if h else yy * 4 + (xx % 2) * 2 + xx // 2

    four = range(4)
    a_unit = jnp.stack([unit((y - s) % 4, x ^ e, 0) for s in four for e in four])
    b_unit = jnp.stack([unit(y ^ e, (x - s) % 4, 1) for s in four for e in four])
    same = jnp.asarray([e for _ in four for e in four], jnp.int32)

    acc = encode(same, a_unit, a, a_oth, w_near, b_dec, None, None, None)
    codes = encode(same, b_unit, b, b_oth, w_near, b_dec, acc, b_enc, dec_norm)
    own_a, oth_a = decode(codes, w_near, 0, 4096)
    got_a = shift(oth_a, "c", 1)
    own_b, oth_b = decode(codes, w_near, 4096, 4096)
    got_b = shift(oth_b, "c", 1)

    h_a = (own_a + got_a.astype(f32)).astype(bf16).reshape(4, 4, 8, 4096)
    h_b = (own_b + got_b.astype(f32)).astype(bf16).reshape(4, 4, 8, 4096)
    r_a = reduce_ring(h_a, "y")
    r_b = reduce_ring(jnp.moveaxis(h_b, 1, 0), "x")
    r_a = reduce_double(r_a, "x")
    r_b = reduce_double(r_b, "y")
    r = jnp.concatenate([r_a, r_b], axis=1).reshape(4, 2, 8192)
    full = reduce_double(r, "z") + b_dec

    codes_s, stream_s, a_s, b_s, _ = lax.optimization_barrier((codes, stream, a, b, own_b))
    idx2 = by_core(lax.iota(jnp.int32, 256))
    where = jnp.concatenate([take(idx2, c), take(idx2, 1 - c)])
    back = (lax.iota(jnp.int32, 256)[:, None] == where[None, :]).astype(bf16)
    codes_out = jnp.dot(back, codes_s, preferred_element_type=f32).astype(bf16)

    s4 = stream_s.reshape(4, 2, own_rows, 1024)
    s_got = shift(take(s4, 1 - xl, 1), "xl", 1)
    s_own = take(s4, xl, 1)
    s_two = jnp.stack([jnp.where(xl == 0, s_own, s_got), jnp.where(xl == 0, s_got, s_own)])
    s_rel = [take(s_two, y, 1)] + [shift(take(s_two, (y + s) % 4, 1), "y", s) for s in (1, 2, 3)]
    s_rel = jnp.stack(s_rel)
    s_abs = [take(s_rel, (y - yy) % 4) for yy in four]
    pieces = [s_abs[yy][xx, :, :512] for yy in four for xx in (0, 1)]
    pieces += [s_abs[yy][xx, :, 512:] for xx in (0, 1) for yy in four]
    stream_out = jnp.concatenate(pieces, axis=1)

    first = (y * 4 + x) * 8 + z * 2
    mine_a = lax.dynamic_slice_in_dim(a_s.reshape(16, 128, 256), first, 2, 1)
    mine_b = lax.dynamic_slice_in_dim(b_s.reshape(16, 128, 256), first, 2, 1)
    mine = jnp.concatenate([mine_a, mine_b])
    places = jnp.concatenate([a_unit, b_unit])
    unsort = (lax.iota(jnp.int32, 32)[:, None] == places[None, :]).astype(bf16)
    mine = jnp.dot(unsort, mine.reshape(32, 512), preferred_element_type=f32)
    mine = mine.reshape(32, 2, 256).transpose(1, 0, 2).reshape(2, 8192)
    error = jnp.mean((full - mine) ** 2, axis=1)
    return stream_out, codes_out, full.astype(bf16), error


def solution(mesh):
    fine = Mesh(mesh.devices.reshape(SIZES), AXES)
    return jax.shard_map(
        shards,
        mesh=fine,
        in_specs=(
            P(LAT, TP),
            P(TP, None),
            P(LAT + TP, None),
            P(),
            P(None, TP + LAT),
            P(TP + LAT),
            P(TP + LAT),
            P(),
        ),
        out_specs=(
            P(LAT + TP, None),
            P(None, TP + LAT),
            P(TP + LAT, None),
            P(TP + LAT),
        ),
        check_vma=False,
    )
```

```python
import jax
import jax.numpy as jnp
from jax import lax
from jax.experimental import pallas as pl
from jax.experimental.pallas import tpu as pltpu
from jax.sharding import Mesh, PartitionSpec as P


AXES = ("y", "xl", "xh", "z", "c")
SIZES = (4, 2, 2, 4, 2)
TP = ("y", "xl")
LAT = ("xh", "z", "c")
bf16 = jnp.bfloat16
f32 = jnp.float32


def _x(i):
    i %= 4
    return (i % 2) * 2 + i // 2


def shift(v, ax, s):
    if ax == "x":
        return lax.ppermute(v, ("xl", "xh"), [(_x(i), _x(i + s)) for i in range(4)])
    n = 4 if ax in "yz" else 2
    return lax.ppermute(v, ax, [(i, (i + s) % n) for i in range(n)])


def coord(ax):
    if ax == "x":
        return lax.axis_index("xh") * 2 + lax.axis_index("xl")
    return lax.axis_index(ax)


def cut(v, starts, sizes):
    return lax.dynamic_slice(v, starts, sizes, allow_negative_indices=False)


def take(v, i, axis=0):
    axis %= v.ndim
    sizes = [1 if a == axis else n for a, n in enumerate(v.shape)]
    return jnp.squeeze(cut(v, [i if a == axis else 0 for a in range(v.ndim)], sizes), axis)


def reduce_ring(v, ax):
    me = coord(ax)
    got = [shift(take(v, (me + s) & 3), ax, s) for s in (2, 1, 3)]
    total = take(v, me).astype(f32)
    for g in got:
        total = total + g.astype(f32)
    return total


def gather_ring(v, ax):
    got = {s: shift(v, ax, s) for s in (2, 1, 3)}
    return jnp.stack([v, got[1], got[2], got[3]])


def swap(v, ax, bit):
    if ax == "x":
        return lax.ppermute(v, ("xl", "xh"), [(_x(i), _x(i ^ bit)) for i in range(4)])
    return lax.ppermute(v, ax, [(i, i ^ bit) for i in range(4)])


def gather_double(v, ax):
    two = jnp.stack([v, swap(v, ax, 1)])
    return jnp.concatenate([two, swap(two, ax, 2)])


def reduce_double(v, ax, bits):
    v = v.reshape((2, 2) + v.shape[1:])
    for bit, axis, (mine, other) in ((1, 1, bits[0]), (2, 0, bits[1])):
        v = take(v, mine, axis) + swap(take(v, other, axis).astype(bf16), ax, bit).astype(f32)
    return v


VM = pl.BlockSpec(memory_space=pltpu.VMEM)
SM = pl.BlockSpec(memory_space=pltpu.SMEM)
HB = pl.BlockSpec(memory_space=pltpu.HBM)


def limit(mib):
    return pltpu.CompilerParams(vmem_limit_bytes=mib * 1024 * 1024)


def hbm(v):
    return pltpu.with_memory_space_constraint(v, pltpu.HBM)


def project(cols, attn, w_out, resid, counts, dtypes):
    rows, inner = attn.shape
    few = resid.shape[0]
    width, steps = 512, sum(counts)

    def kernel(cols_ref, attn_hbm, w_ref, r_hbm, *rest):
        outs, (attn_ref, r_ref, buf, sems) = rest[:-4], rest[-4:]

        def span(i):
            return pl.ds(pl.multiple_of(cols_ref[i] * width, width), width)

        small = [
            pltpu.make_async_copy(attn_hbm, attn_ref, sems.at[steps]),
            pltpu.make_async_copy(r_hbm, r_ref, sems.at[steps + 1]),
        ]
        copies = [pltpu.make_async_copy(w_ref.at[:, span(i)], buf.at[i], sems.at[i]) for i in range(steps)]
        for copy in small + copies:
            copy.start()
        at = lax.broadcasted_iota(jnp.int32, (rows, few), 0) - cols_ref[3 * steps] * few
        place = jnp.where(at == lax.broadcasted_iota(jnp.int32, (rows, few), 1), 1.0, 0.0).astype(bf16)
        for copy in small:
            copy.wait()
        slots = [(o, j) for o, n in zip(outs, counts) for j in range(n)]
        for i, (o, j) in enumerate(slots):
            copies[i].wait()
            acc = jnp.dot(attn_ref[...], buf[i], preferred_element_type=f32)
            acc = acc + jnp.dot(place, r_ref[:, span(i)], preferred_element_type=f32)
            o[j] = acc.astype(o.dtype)

    return pl.pallas_call(
        kernel,
        in_specs=[SM, HB, HB, HB],
        out_specs=[VM] * len(counts),
        out_shape=[jax.ShapeDtypeStruct((n, rows, width), d) for n, d in zip(counts, dtypes)],
        scratch_shapes=[
            pltpu.VMEM(attn.shape, bf16),
            pltpu.VMEM(resid.shape, bf16),
            pltpu.VMEM((steps, inner, width), bf16),
            pltpu.SemaphoreType.DMA((steps + 2,)),
        ],
        compiler_params=limit(12),
        name="project",
    )(cols, hbm(attn), hbm(w_out), hbm(resid))


def autoencode(table, skip, own_a, oth_a, own_b, oth_b, w_enc, b_dec, b_enc, dec_norm, back):
    half, width = own_a.shape[2:]
    d_model, lat = w_enc.shape
    n = d_model // width
    per = n // 2
    split = d_model // 2
    out_width = 512

    def kernel(table_ref, oa_ref, ta_ref, ob_ref, tb_ref, w_ref, bd_ref, be_ref, dn_ref, back_ref, codes_ref, *rest):
        outs, (buf, sems) = rest[:4], rest[4:]

        def span(j):
            return pl.ds(pl.multiple_of(table_ref[skip + j] * width, width), width)

        copies = [pltpu.make_async_copy(w_ref.at[span(j)], buf.at[span(j)], sems.at[j]) for j in range(n)]
        for copy in copies:
            copy.start()
        total = None
        for h, (o_ref, t_ref) in enumerate(((oa_ref, ta_ref), (ob_ref, tb_ref))):
            for j in range(h * per, (h + 1) * per):
                i, k = j // 4 % 4, j % 4
                lhs = jnp.concatenate([o_ref[i, k], t_ref[i, k]], axis=0)
                lhs = (lhs.astype(f32) - bd_ref[table_ref[skip + j]]).astype(bf16)
                copies[j].wait()
                term = jnp.dot(lhs, buf[span(j)], preferred_element_type=f32)
                total = term if total is None else total + term
        pre = total + be_ref[...]
        codes = (jnp.maximum(pre, 0.0) * dn_ref[...]).astype(bf16)
        codes_ref[...] = jnp.dot(back_ref[...], codes, preferred_element_type=f32).astype(bf16)
        for i in range(d_model // out_width):
            own_ref, oth_ref = outs[:2] if i * out_width < split else outs[2:]
            first = i * out_width % split
            to = slice(first, first + out_width)
            w = buf[i * out_width : (i + 1) * out_width]
            r = lax.dot_general(codes, w, (((1,), (1,)), ((), ())), preferred_element_type=f32)
            own_ref[:, to] = r[:half]
            oth_ref[:, to] = r[half:].astype(bf16)

    own_shape = jax.ShapeDtypeStruct((half, split), f32)
    oth_shape = jax.ShapeDtypeStruct((half, split), bf16)
    return pl.pallas_call(
        kernel,
        in_specs=[SM, VM, VM, VM, VM, HB, VM, VM, VM, VM],
        out_specs=[VM] * 5,
        out_shape=[jax.ShapeDtypeStruct((2 * half, lat), bf16), own_shape, oth_shape, own_shape, oth_shape],
        scratch_shapes=[pltpu.VMEM((d_model, lat), bf16), pltpu.SemaphoreType.DMA((n,))],
        compiler_params=limit(22),
        name="autoencode",
    )(table, own_a, oth_a, own_b, oth_b, hbm(w_enc), b_dec.reshape(-1, 1, width), b_enc[None], dec_norm[None], back)


def step(attn_out, w_out, resid_in, positions, w_enc, b_enc, dec_norm, b_dec):
    y, xl, xh, z, c = (lax.axis_index(a) for a in AXES)
    x = coord("x")
    t = y * 2 + xl
    lat = xh * 8 + z * 2 + c
    own_rows = resid_in.shape[0]
    rows = attn_out.shape[0]

    def block(dy, dx, h):
        yy, xx = (y + dy) & 3, xl ^ dx
        return 8 + xx * 4 + yy if h else yy * 2 + xx

    cols = [block(dy, 1, 0) for dy in range(4)] + [block(dy, dx, 1) for dy in (2, 1, 3) for dx in (0, 1)]
    cols += [block(dy, 0, 0) for dy in range(4)] + [block(0, dx, 1) for dx in (0, 1)]

    def unit(yy, xx, h):
        return 16 + (xx & 1) * 8 + yy * 2 + (xx >> 1) if h else yy * 4 + (xx & 1) * 2 + (xx >> 1)

    four = range(4)
    units = [unit((y - s) & 3, x ^ e, 0) for s in four for e in four]
    units += [unit(y ^ e, (x - s) & 3, 1) for s in four for e in four]
    first = (y * 4 + x) * 8 + z * 2
    later = [(i + s) & 3 for i in (x, y, z) for s in four] + [(y - s) & 3 for s in four]
    y_bits = tuple((b, b ^ 1) for b in (y & 1, y >> 1))
    later += [b for pair in y_bits for b in pair] + [c, c ^ 1, xh, xh ^ 1, xl, xl ^ 1, x, y, z, first]
    homes = [((y - yy) & 3) * 2 + (xl ^ xx) for yy in four for xx in (0, 1)]
    later += homes
    table = lax.optimization_barrier(jnp.stack(cols + units + [t] + later))
    a_send, b2, b1, b3, a_keep, b_keep = project(
        table, attn_out, w_out, resid_in, (4, 2, 2, 2, 4, 2), (bf16,) * 4 + (f32,) * 2
    )
    a_got = shift(a_send, "xl", 1)
    b_got = [shift(b2, "y", 2), shift(b1, "y", 1), shift(b3, "y", 3)]
    a_more = [shift((a_keep[s] + a_got[s].astype(f32)).astype(bf16), "y", s) for s in (2, 1, 3)]

    def b_part(dx):
        return b_keep[dx] + b_got[0][dx].astype(f32) + b_got[1][dx].astype(f32) + b_got[2][dx].astype(f32)

    b_more = shift(b_part(1).astype(bf16), "xl", 1)
    a_sum = a_keep[0] + a_got[0].astype(f32)
    for g in a_more:
        a_sum = a_sum + g.astype(f32)
    b_sum = b_part(0) + b_more.astype(f32)
    stream = jnp.concatenate([a_sum, b_sum], axis=1).astype(bf16)

    def by_core(v):
        return v.reshape(4, 2, 2, 4, 2, 2).transpose(4, 0, 2, 1, 3, 5).reshape(2, 128)

    pos2 = by_core(positions)
    ids = lat * rows + lax.iota(jnp.int32, rows)

    def hot(p):
        return (p[:, None] == ids[None, :]).astype(bf16)

    def pick(h, s):
        return jnp.dot(h, s, preferred_element_type=f32).astype(bf16)

    hot_own, hot_oth = hot(take(pos2, c)), hot(take(pos2, c ^ 1))
    parts = stream.reshape(rows, 2, 2, 256)
    cut_own, cut_oth = (take(parts, i, 2).reshape(rows, 512) for i in (xh, xh ^ 1))
    both = lax.ppermute(pick(hot_oth, cut_oth), ("xh", "c"), [(i, i ^ 3) for i in range(4)])
    other_h = shift(pick(hot_own, cut_oth), "xh", 1)
    other_c = shift(pick(hot_oth, cut_own), "c", 1)
    v = pick(hot_own, cut_own) + both + other_h + other_c
    got = [shift(v, "z", s) for s in (2, 1, 3)]
    v = v + got[0] + got[1] + got[2]
    s4 = stream.reshape(4, 2, own_rows, 1024)
    s_got = shift(take(s4, xl ^ 1, 1), "xl", 1)
    v, s_got = lax.optimization_barrier((v, s_got))
    v = v.reshape(rows, 2, 256)

    a = gather_double(v[:, 0], "x")
    b = gather_double(v[:, 1], "y")
    a = gather_ring(a, "y")
    b = gather_ring(b, "x")
    a_oth = shift(a, "c", 1)
    b_oth = shift(b, "c", 1)

    idx2 = by_core(lax.iota(jnp.int32, 256))
    where = jnp.concatenate([take(idx2, c), take(idx2, c ^ 1)])
    back = (lax.iota(jnp.int32, 256)[:, None] == where[None, :]).astype(bf16)
    codes_out, own_a, oth_a, own_b, oth_b = autoencode(
        table, len(cols), a, a_oth, b, b_oth, w_enc, b_dec, b_enc, dec_norm, back
    )
    got_a = shift(oth_a, "c", 1)
    got_b = shift(oth_b, "c", 1)

    h_a = (own_a + got_a.astype(f32)).astype(bf16).reshape(4, 4, 8, 4096)
    h_b = (own_b + got_b.astype(f32)).astype(bf16).reshape(4, 4, 8, 4096)
    r_a = reduce_ring(h_a, "y")
    r_b = reduce_ring(jnp.moveaxis(h_b, 1, 0), "x")
    r_a = reduce_double(r_a, "x", ((xl, xl ^ 1), (xh, xh ^ 1)))
    r_b = reduce_double(r_b, "y", y_bits)
    r = jnp.concatenate([r_a, r_b], axis=1).astype(bf16).reshape(4, 2, 8192)
    full = reduce_ring(r, "z") + b_dec

    a_s, b_s, _ = lax.optimization_barrier((a, b, own_b))
    s_own = take(s4, xl, 1)
    s_two = jnp.stack([s_own, s_got])
    s_rel = [take(s_two, y, 1)] + [shift(take(s_two, (y + s) & 3, 1), "y", s) for s in (1, 2, 3)]
    s_rel = jnp.stack(s_rel).reshape(8, own_rows, 1024)

    def home(yy, xx, h):
        return take(s_rel[:, :, h * 512 : (h + 1) * 512], homes[yy * 2 + xx])

    pieces = [home(yy, xx, 0) for yy in four for xx in (0, 1)]
    pieces += [home(yy, xx, 1) for xx in (0, 1) for yy in four]
    stream_out = jnp.concatenate(pieces, axis=1)

    mine_a, mine_b = (cut(v.reshape(16, 128, 256), (0, first, 0), (16, 2, 256)) for v in (a_s, b_s))
    mine = jnp.concatenate([mine_a, mine_b])
    places = table[len(cols) : len(cols) + 32]
    unsort = (lax.iota(jnp.int32, 32)[:, None] == places[None, :]).astype(bf16)
    mine = jnp.dot(unsort, mine.reshape(32, 512), preferred_element_type=f32)
    mine = mine.reshape(32, 2, 256).transpose(1, 0, 2).reshape(2, 8192)
    error = jnp.mean((full - mine) ** 2, axis=1)
    return stream_out, codes_out, full.astype(bf16), error


def solution(mesh):
    fine = Mesh(mesh.devices.reshape(SIZES), AXES)
    return jax.shard_map(
        step,
        mesh=fine,
        in_specs=(
            P(LAT, TP),
            P(TP, None),
            P(LAT + TP, None),
            P(),
            P(None, TP + LAT),
            P(TP + LAT),
            P(TP + LAT),
            P(),
        ),
        out_specs=(
            P(LAT + TP, None),
            P(None, TP + LAT),
            P(TP + LAT, None),
            P(TP + LAT),
        ),
        check_vma=False,
    )
```

```python
import jax
import jax.numpy as jnp
from jax import lax
from jax.experimental import pallas as pl
from jax.experimental.pallas import tpu as pltpu
from jax.sharding import Mesh, PartitionSpec as P


AXES = ("y", "xl", "xh", "z", "c")
SIZES = (4, 2, 2, 4, 2)
TP = ("y", "xl")
LAT = ("xh", "z", "c")
bf16 = jnp.bfloat16
f32 = jnp.float32


def _x(i):
    i %= 4
    return (i % 2) * 2 + i // 2


def shift(v, ax, s):
    if ax == "x":
        return lax.ppermute(v, ("xl", "xh"), [(_x(i), _x(i + s)) for i in range(4)])
    n = 4 if ax in "yz" else 2
    return lax.ppermute(v, ax, [(i, (i + s) % n) for i in range(n)])


def coord(ax):
    if ax == "x":
        return lax.axis_index("xh") * 2 + lax.axis_index("xl")
    return lax.axis_index(ax)


def cut(v, starts, sizes):
    return lax.dynamic_slice(v, starts, sizes, allow_negative_indices=False)


def take(v, i, axis=0):
    axis %= v.ndim
    sizes = [1 if a == axis else n for a, n in enumerate(v.shape)]
    return jnp.squeeze(cut(v, [i if a == axis else 0 for a in range(v.ndim)], sizes), axis)


def reduce_ring(v, ax):
    me = coord(ax)
    got = [shift(take(v, (me + s) & 3), ax, s) for s in (2, 1, 3)]
    total = take(v, me).astype(f32)
    for g in got:
        total = total + g.astype(f32)
    return total


def gather_ring(v, ax):
    got = {s: shift(v, ax, s) for s in (2, 1, 3)}
    return jnp.stack([v, got[1], got[2], got[3]])


def swap(v, ax, bit):
    if ax == "x":
        return lax.ppermute(v, ("xl", "xh"), [(_x(i), _x(i ^ bit)) for i in range(4)])
    return lax.ppermute(v, ax, [(i, i ^ bit) for i in range(4)])


def gather_double(v, ax):
    two = jnp.stack([v, swap(v, ax, 1)])
    return jnp.concatenate([two, swap(two, ax, 2)])


def reduce_double(v, ax, bits):
    v = v.reshape((2, 2) + v.shape[1:])
    for bit, axis, (mine, other) in ((1, 1, bits[0]), (2, 0, bits[1])):
        v = take(v, mine, axis) + swap(take(v, other, axis).astype(bf16), ax, bit).astype(f32)
    return v


VM = pl.BlockSpec(memory_space=pltpu.VMEM)
SM = pl.BlockSpec(memory_space=pltpu.SMEM)
HB = pl.BlockSpec(memory_space=pltpu.HBM)


def limit(mib):
    return pltpu.CompilerParams(vmem_limit_bytes=mib * 1024 * 1024)


def hbm(v):
    return pltpu.with_memory_space_constraint(v, pltpu.HBM)


def project(table, skip, place_at, attn, w_out, resid, counts, dtypes):
    rows, inner = attn.shape
    few = resid.shape[0]
    width, steps = 512, sum(counts)

    def kernel(table_ref, attn_hbm, w_ref, r_hbm, *rest):
        outs, (attn_ref, r_ref, buf, sems) = rest[:-4], rest[-4:]

        def span(i):
            return pl.ds(pl.multiple_of(table_ref[skip + i] * width, width), width)

        small = [
            pltpu.make_async_copy(attn_hbm, attn_ref, sems.at[steps]),
            pltpu.make_async_copy(r_hbm, r_ref, sems.at[steps + 1]),
        ]
        copies = [pltpu.make_async_copy(w_ref.at[:, span(i)], buf.at[i], sems.at[i]) for i in range(steps)]
        for copy in small + copies:
            copy.start()
        at = lax.broadcasted_iota(jnp.int32, (rows, few), 0) - table_ref[place_at] * few
        place = jnp.where(at == lax.broadcasted_iota(jnp.int32, (rows, few), 1), 1.0, 0.0).astype(bf16)
        for copy in small:
            copy.wait()
        slots = [(o, j) for o, n in zip(outs, counts) for j in range(n)]
        for i, (o, j) in enumerate(slots):
            copies[i].wait()
            acc = jnp.dot(attn_ref[...], buf[i], preferred_element_type=f32)
            acc = acc + jnp.dot(place, r_ref[:, span(i)], preferred_element_type=f32)
            o[j] = acc.astype(o.dtype)

    return pl.pallas_call(
        kernel,
        in_specs=[SM, HB, HB, HB],
        out_specs=[VM] * len(counts),
        out_shape=[jax.ShapeDtypeStruct((n, rows, width), d) for n, d in zip(counts, dtypes)],
        scratch_shapes=[
            pltpu.VMEM(attn.shape, bf16),
            pltpu.VMEM(resid.shape, bf16),
            pltpu.VMEM((steps, inner, width), bf16),
            pltpu.SemaphoreType.DMA((steps + 2,)),
        ],
        compiler_params=limit(12),
        name="project",
    )(table, hbm(attn), hbm(w_out), hbm(resid))


def autoencode(table, skip, own_a, oth_a, own_b, oth_b, w_enc, b_dec, b_enc, dec_norm, back):
    half, width = own_a.shape[2:]
    d_model, lat = w_enc.shape
    n = d_model // width
    per = n // 2
    split = d_model // 2
    out_width = 512

    def kernel(table_ref, oa_ref, ta_ref, ob_ref, tb_ref, w_ref, bd_ref, be_ref, dn_ref, back_ref, codes_ref, *rest):
        outs, (buf, sems) = rest[:4], rest[4:]

        def span(j):
            return pl.ds(pl.multiple_of(table_ref[skip + j] * width, width), width)

        copies = [pltpu.make_async_copy(w_ref.at[span(j)], buf.at[span(j)], sems.at[j]) for j in range(n)]
        for copy in copies:
            copy.start()
        total = None
        for h, (o_ref, t_ref) in enumerate(((oa_ref, ta_ref), (ob_ref, tb_ref))):
            for j in range(h * per, (h + 1) * per):
                i, k = j // 4 % 4, j % 4
                lhs = jnp.concatenate([o_ref[i, k], t_ref[i, k]], axis=0)
                lhs = (lhs.astype(f32) - bd_ref[table_ref[skip + j]]).astype(bf16)
                copies[j].wait()
                term = jnp.dot(lhs, buf[span(j)], preferred_element_type=f32)
                total = term if total is None else total + term
        pre = total + be_ref[...]
        codes = (jnp.maximum(pre, 0.0) * dn_ref[...]).astype(bf16)
        codes_ref[...] = jnp.dot(back_ref[...], codes, preferred_element_type=f32).astype(bf16)
        for i in range(d_model // out_width):
            own_ref, oth_ref = outs[:2] if i * out_width < split else outs[2:]
            first = i * out_width % split
            to = slice(first, first + out_width)
            w = buf[i * out_width : (i + 1) * out_width]
            r = lax.dot_general(codes, w, (((1,), (1,)), ((), ())), preferred_element_type=f32)
            own_ref[:, to] = r[:half]
            oth_ref[:, to] = r[half:].astype(bf16)

    own_shape = jax.ShapeDtypeStruct((half, split), f32)
    oth_shape = jax.ShapeDtypeStruct((half, split), bf16)
    return pl.pallas_call(
        kernel,
        in_specs=[SM, VM, VM, VM, VM, HB, VM, VM, VM, VM],
        out_specs=[VM] * 5,
        out_shape=[jax.ShapeDtypeStruct((2 * half, lat), bf16), own_shape, oth_shape, own_shape, oth_shape],
        scratch_shapes=[pltpu.VMEM((d_model, lat), bf16), pltpu.SemaphoreType.DMA((n,))],
        compiler_params=limit(22),
        name="autoencode",
    )(table, own_a, oth_a, own_b, oth_b, hbm(w_enc), b_dec.reshape(-1, 1, width), b_enc[None], dec_norm[None], back)


def step(attn_out, w_out, resid_in, positions, w_enc, b_enc, dec_norm, b_dec):
    y, xl, xh, z, c = (lax.axis_index(a) for a in AXES)
    x = coord("x")
    t = y * 2 + xl
    lat = xh * 8 + z * 2 + c
    own_rows = resid_in.shape[0]
    rows = attn_out.shape[0]

    def block(dy, dx, h):
        yy, xx = (y + dy) & 3, xl ^ dx
        return 8 + xx * 4 + yy if h else yy * 2 + xx

    cols = [block(dy, 1, 0) for dy in range(4)] + [block(dy, dx, 1) for dy in (2, 1, 3) for dx in (0, 1)]
    cols += [block(dy, 0, 0) for dy in range(4)] + [block(0, dx, 1) for dx in (0, 1)]

    def unit(yy, xx, h):
        return 16 + (xx & 1) * 8 + yy * 2 + (xx >> 1) if h else yy * 4 + (xx & 1) * 2 + (xx >> 1)

    four = range(4)
    units = [unit((y - s) & 3, x ^ e, 0) for s in four for e in four]
    units += [unit(y ^ e, (x - s) & 3, 1) for s in four for e in four]
    first = (y * 4 + x) * 8 + z * 2
    later = [(i + s) & 3 for i in (x, y, z) for s in four] + [(y - s) & 3 for s in four]
    y_bits = tuple((b, b ^ 1) for b in (y & 1, y >> 1))
    later += [b for pair in y_bits for b in pair] + [c, c ^ 1, xh, xh ^ 1, xl, xl ^ 1, x, y, z, first]
    homes = [((y - yy) & 3) * 2 + (xl ^ xx) for yy in four for xx in (0, 1)]
    base = lat * rows
    two_own, two_oth = c * 2, (c ^ 1) * 2
    later += homes + [base, two_own, two_oth]
    table = lax.optimization_barrier(jnp.stack(cols + units + [t] + later))
    place_at = len(cols) + len(units)
    a_send, b2, b1, b3 = project(table, 0, place_at, attn_out, w_out, resid_in, (4, 2, 2, 2), (bf16,) * 4)
    a_got = shift(a_send, "xl", 1)
    b_got = [shift(b2, "y", 2), shift(b1, "y", 1), shift(b3, "y", 3)]
    a_keep, b_keep = project(table, 10, place_at, attn_out, w_out, resid_in, (4, 2), (f32,) * 2)
    a_more = [shift((a_keep[s] + a_got[s].astype(f32)).astype(bf16), "y", s) for s in (2, 1, 3)]

    def b_part(dx):
        return b_keep[dx] + b_got[0][dx].astype(f32) + b_got[1][dx].astype(f32) + b_got[2][dx].astype(f32)

    b_more = shift(b_part(1).astype(bf16), "xl", 1)
    a_sum = a_keep[0] + a_got[0].astype(f32)
    for g in a_more:
        a_sum = a_sum + g.astype(f32)
    b_sum = b_part(0) + b_more.astype(f32)
    stream = jnp.concatenate([a_sum, b_sum], axis=1).astype(bf16)

    def template_row(r, two_core):
        xx = (r >> 3) & 3
        return (r >> 5) * 64 + (xx & 1) * 32 + (xx >> 1) * 16 + ((r >> 1) & 3) * 4 + two_core + (r & 1)

    def iota(shape, axis):
        return lax.broadcasted_iota(jnp.int32, shape, axis)

    hits = (iota((rows, 256), 0) + base == positions[None, :]).astype(bf16)

    def hot(two_core):
        rank = (template_row(iota((128, 256), 0), two_core) == iota((128, 256), 1)).astype(bf16)
        return lax.dot_general(rank, hits, (((1,), (1,)), ((), ())), preferred_element_type=f32).astype(bf16)

    def pick(h, s):
        return jnp.dot(h, s, preferred_element_type=f32).astype(bf16)

    v = pick(hot(two_own), stream) + shift(pick(hot(two_oth), stream), "c", 1)
    v = v.reshape(rows, 2, 2, 256)
    v = take(v, xh, 2) + shift(take(v, xh ^ 1, 2), "xh", 1)
    for bit in (1, 2):
        v = v + swap(v, "z", bit)
    v = v.reshape(rows, 2, 256)

    a = gather_double(v[:, 0], "x")
    b = gather_double(v[:, 1], "y")
    a = gather_ring(a, "y")
    b = gather_ring(b, "x")
    s4 = stream.reshape(4, 2, own_rows, 1024)
    s_got = shift(take(s4, xl ^ 1, 1), "xl", 1)
    a, s_got = lax.optimization_barrier((a, s_got))
    a_oth = shift(a, "c", 1)
    b_oth = shift(b, "c", 1)

    k = iota((256, 256), 1)
    back = (iota((256, 256), 0) == template_row(k & 127, two_own ^ ((k >> 7) * 2))).astype(bf16)
    codes_out, own_a, oth_a, own_b, oth_b = autoencode(
        table, len(cols), a, a_oth, b, b_oth, w_enc, b_dec, b_enc, dec_norm, back
    )
    got_a = shift(oth_a, "c", 1)
    got_b = shift(oth_b, "c", 1)

    h_a = (own_a + got_a.astype(f32)).astype(bf16).reshape(4, 4, 8, 4096)
    h_b = (own_b + got_b.astype(f32)).astype(bf16).reshape(4, 4, 8, 4096)
    r_a = reduce_ring(h_a, "y")
    r_b = reduce_ring(jnp.moveaxis(h_b, 1, 0), "x")
    r_a = reduce_double(r_a, "x", ((xl, xl ^ 1), (xh, xh ^ 1)))
    r_b = reduce_double(r_b, "y", y_bits)
    r = jnp.concatenate([r_a, r_b], axis=1).astype(bf16).reshape(4, 2, 8192)
    full = reduce_ring(r, "z") + b_dec

    a_s, b_s, _ = lax.optimization_barrier((a, b, own_b))
    s_own = take(s4, xl, 1)
    s_two = jnp.stack([s_own, s_got])
    s_rel = [shift(take(s_two, (y + s) & 3, 1), "y", s) for s in (1, 2, 3)]
    *s_rel, _ = lax.optimization_barrier((*s_rel, r))
    s_rel = [take(s_two, y, 1)] + s_rel
    s_rel = jnp.stack(s_rel).reshape(8, own_rows, 1024)

    def home(yy, xx, h):
        return take(s_rel[:, :, h * 512 : (h + 1) * 512], homes[yy * 2 + xx])

    pieces = [home(yy, xx, 0) for yy in four for xx in (0, 1)]
    pieces += [home(yy, xx, 1) for xx in (0, 1) for yy in four]
    stream_out = jnp.concatenate(pieces, axis=1)

    mine_a, mine_b = (cut(v.reshape(16, 128, 256), (0, first, 0), (16, 2, 256)) for v in (a_s, b_s))
    mine = jnp.concatenate([mine_a, mine_b])
    places = table[len(cols) : len(cols) + 32]
    unsort = (lax.iota(jnp.int32, 32)[:, None] == places[None, :]).astype(bf16)
    mine = jnp.dot(unsort, mine.reshape(32, 512), preferred_element_type=f32)
    mine = mine.reshape(32, 2, 256).transpose(1, 0, 2).reshape(2, 8192)
    error = jnp.mean((full - mine) ** 2, axis=1)
    return stream_out, codes_out, full.astype(bf16), error


def solution(mesh):
    fine = Mesh(mesh.devices.reshape(SIZES), AXES)
    return jax.shard_map(
        step,
        mesh=fine,
        in_specs=(
            P(LAT, TP),
            P(TP, None),
            P(LAT + TP, None),
            P(),
            P(None, TP + LAT),
            P(TP + LAT),
            P(TP + LAT),
            P(),
        ),
        out_specs=(
            P(LAT + TP, None),
            P(None, TP + LAT),
            P(TP + LAT, None),
            P(TP + LAT),
        ),
        check_vma=False,
    )
```

```python
import jax
import jax.numpy as jnp
from jax import lax
from jax.experimental import pallas as pl
from jax.experimental.pallas import tpu as pltpu
from jax.sharding import Mesh, PartitionSpec as P


AXES = ("y", "xl", "xh", "z", "c")
SIZES = (4, 2, 2, 4, 2)
TP = ("y", "xl")
LAT = ("xh", "z", "c")
bf16 = jnp.bfloat16
f32 = jnp.float32


def _x(i):
    i %= 4
    return (i % 2) * 2 + i // 2


def shift(v, ax, s):
    if ax == "x":
        return lax.ppermute(v, ("xl", "xh"), [(_x(i), _x(i + s)) for i in range(4)])
    n = 4 if ax in "yz" else 2
    return lax.ppermute(v, ax, [(i, (i + s) % n) for i in range(n)])


def coord(ax):
    if ax == "x":
        return lax.axis_index("xh") * 2 + lax.axis_index("xl")
    return lax.axis_index(ax)


def cut(v, starts, sizes):
    return lax.dynamic_slice(v, starts, sizes, allow_negative_indices=False)


def take(v, i, axis=0):
    axis %= v.ndim
    sizes = [1 if a == axis else n for a, n in enumerate(v.shape)]
    return jnp.squeeze(cut(v, [i if a == axis else 0 for a in range(v.ndim)], sizes), axis)


def reduce_ring(v, ax):
    me = coord(ax)
    got = [shift(take(v, (me + s) & 3), ax, s) for s in (2, 1, 3)]
    total = take(v, me).astype(f32)
    for g in got:
        total = total + g.astype(f32)
    return total


def gather_ring(v, ax):
    got = {s: shift(v, ax, s) for s in (2, 1, 3)}
    return jnp.stack([got[1], got[2], got[3]])


def swap(v, ax, bit):
    if ax == "x":
        return lax.ppermute(v, ("xl", "xh"), [(_x(i), _x(i ^ bit)) for i in range(4)])
    return lax.ppermute(v, ax, [(i, i ^ bit) for i in range(4)])


def gather_double(v, ax):
    two = jnp.stack([v, swap(v, ax, 1)])
    return jnp.concatenate([two, swap(two, ax, 2)])


def reduce_double(v, ax, bits):
    v = v.reshape((2, 2) + v.shape[1:])
    for bit, axis, (mine, other) in ((1, 1, bits[0]), (2, 0, bits[1])):
        v = take(v, mine, axis) + swap(take(v, other, axis).astype(bf16), ax, bit).astype(f32)
    return v


VM = pl.BlockSpec(memory_space=pltpu.VMEM)
SM = pl.BlockSpec(memory_space=pltpu.SMEM)
HB = pl.BlockSpec(memory_space=pltpu.HBM)


def limit(mib):
    return pltpu.CompilerParams(vmem_limit_bytes=mib * 1024 * 1024)


def hbm(v):
    return pltpu.with_memory_space_constraint(v, pltpu.HBM)


def project(table, skip, place_at, attn, w_out, resid, counts, dtypes):
    rows, inner = attn.shape
    few = resid.shape[0]
    width, steps = 512, sum(counts)

    def kernel(table_ref, attn_hbm, w_ref, r_hbm, *rest):
        outs, (attn_ref, r_ref, buf, sems) = rest[:-4], rest[-4:]

        def span(i):
            return pl.ds(pl.multiple_of(table_ref[skip + i] * width, width), width)

        small = [
            pltpu.make_async_copy(attn_hbm, attn_ref, sems.at[steps]),
            pltpu.make_async_copy(r_hbm, r_ref, sems.at[steps + 1]),
        ]
        copies = [pltpu.make_async_copy(w_ref.at[:, span(i)], buf.at[i], sems.at[i]) for i in range(steps)]
        for copy in small + copies:
            copy.start()
        at = lax.broadcasted_iota(jnp.int32, (rows, few), 0) - table_ref[place_at] * few
        place = jnp.where(at == lax.broadcasted_iota(jnp.int32, (rows, few), 1), 1.0, 0.0).astype(bf16)
        for copy in small:
            copy.wait()
        slots = [(o, j) for o, n in zip(outs, counts) for j in range(n)]
        for i, (o, j) in enumerate(slots):
            copies[i].wait()
            acc = jnp.dot(attn_ref[...], buf[i], preferred_element_type=f32)
            acc = acc + jnp.dot(place, r_ref[:, span(i)], preferred_element_type=f32)
            o[j] = acc.astype(o.dtype)

    return pl.pallas_call(
        kernel,
        in_specs=[SM, HB, HB, HB],
        out_specs=[VM] * len(counts),
        out_shape=[jax.ShapeDtypeStruct((n, rows, width), d) for n, d in zip(counts, dtypes)],
        scratch_shapes=[
            pltpu.VMEM(attn.shape, bf16),
            pltpu.VMEM(resid.shape, bf16),
            pltpu.VMEM((steps, inner, width), bf16),
            pltpu.SemaphoreType.DMA((steps + 2,)),
        ],
        compiler_params=limit(12),
        name="project",
    )(table, hbm(attn), hbm(w_out), hbm(resid))


def add_terms(total, table_ref, bd_ref, buf, copies, slots):
    for (own, oth, j, rows), copy in zip(slots, copies):
        lhs = jnp.concatenate([own(), oth()], axis=0)
        lhs = (lhs.astype(f32) - bd_ref[table_ref[j]]).astype(bf16)
        copy.wait()
        term = jnp.dot(lhs, buf[rows], preferred_element_type=f32)
        total = term if total is None else total + term
    return total


def first_terms(table, skip, own, oth, w_enc, b_dec):
    half, width = own.shape[2:]
    lat = w_enc.shape[1]
    n = 8

    def kernel(table_ref, own_ref, oth_ref, w_ref, bd_ref, out_ref, buf, sems):
        slots, copies = [], []
        for i in range(n):
            h, k = i // 4, i % 4
            j = skip + 16 * h + k
            rows = pl.ds(pl.multiple_of(table_ref[j] * width, width), width)
            copies.append(pltpu.make_async_copy(w_ref.at[rows], buf.at[pl.ds(i * width, width)], sems.at[i]))
            slots.append((lambda h=h, k=k: own_ref[h, k], lambda h=h, k=k: oth_ref[h, k], j, pl.ds(i * width, width)))
        for copy in copies:
            copy.start()
        out_ref[...] = add_terms(None, table_ref, bd_ref, buf, copies, slots)

    return pl.pallas_call(
        kernel,
        in_specs=[SM, VM, VM, HB, VM],
        out_specs=VM,
        out_shape=jax.ShapeDtypeStruct((2 * half, lat), f32),
        scratch_shapes=[pltpu.VMEM((n * width, lat), bf16), pltpu.SemaphoreType.DMA((n,))],
        compiler_params=limit(12),
        name="first_terms",
    )(table, own, oth, hbm(w_enc), b_dec.reshape(-1, 1, width))


def decode_half(codes, w_ref, own_ref, oth_ref, half):
    width = 512
    for i in range(w_ref.shape[0] // width):
        at = slice(i * width, (i + 1) * width)
        r = lax.dot_general(codes, w_ref[at], (((1,), (1,)), ((), ())), preferred_element_type=f32)
        own_ref[:, at] = r[:half]
        oth_ref[:, at] = r[half:].astype(bf16)


def autoencode(table, skip, acc, own_a, oth_a, own_b, oth_b, w_enc, b_dec, b_enc, dec_norm, back):
    half, width = own_a.shape[2:]
    d_model, lat = w_enc.shape
    n = d_model // width
    per = n // 2
    split = d_model // 2

    def kernel(table_ref, acc_ref, oa_ref, ta_ref, ob_ref, tb_ref, w_ref, bd_ref, be_ref, dn_ref, back_ref, *rest):
        codes_ref, sorted_ref, own_ref, oth_ref, hi_ref, lo_ref, sems = rest

        def fetch(j):
            h = j // per
            unit = table_ref[skip + j]
            local = pl.ds(pl.multiple_of((unit - h * per) * width, width), width)
            rows = pl.ds(pl.multiple_of(unit * width, width), width)
            return pltpu.make_async_copy(w_ref.at[rows], (lo_ref, hi_ref)[h].at[local], sems.at[j]), local

        order = [h * per + j for h in range(2) for j in range(4, per)]
        order += [h * per + j for h in range(2) for j in range(4)]
        made = {j: fetch(j) for j in order}
        for j in order:
            made[j][0].start()
        total = acc_ref[...]
        for h, (o_ref, t_ref, buf) in enumerate(((oa_ref, ta_ref, lo_ref), (ob_ref, tb_ref, hi_ref))):
            mine = range(h * per + 4, (h + 1) * per)
            slots = []
            for j in mine:
                i, k = j // 4 % 4 - 1, j % 4
                slots.append((lambda o=o_ref, i=i, k=k: o[i, k], lambda t=t_ref, i=i, k=k: t[i, k], skip + j, made[j][1]))
            total = add_terms(total, table_ref, bd_ref, buf, [made[j][0] for j in mine], slots)
        for j in order[-8:]:
            made[j][0].wait()
        pre = total + be_ref[...]
        codes = (jnp.maximum(pre, 0.0) * dn_ref[...]).astype(bf16)
        codes_ref[...] = codes
        sorted_ref[...] = jnp.dot(back_ref[...], codes, preferred_element_type=f32).astype(bf16)
        decode_half(codes, lo_ref, own_ref, oth_ref, half)

    codes_shape = jax.ShapeDtypeStruct((2 * half, lat), bf16)
    return pl.pallas_call(
        kernel,
        in_specs=[SM, VM, VM, VM, VM, VM, HB, VM, VM, VM, VM],
        out_specs=[VM] * 5,
        out_shape=[
            codes_shape,
            codes_shape,
            jax.ShapeDtypeStruct((half, split), f32),
            jax.ShapeDtypeStruct((half, split), bf16),
            jax.ShapeDtypeStruct((split, lat), bf16),
        ],
        scratch_shapes=[pltpu.VMEM((split, lat), bf16), pltpu.SemaphoreType.DMA((n,))],
        compiler_params=limit(20),
        name="autoencode",
    )(table, acc, own_a, oth_a, own_b, oth_b, hbm(w_enc), b_dec.reshape(-1, 1, width), b_enc[None], dec_norm[None], back)


def decode(codes, w):
    half, n = codes.shape[0] // 2, w.shape[0]

    def kernel(codes_ref, w_ref, own_ref, oth_ref):
        decode_half(codes_ref[...], w_ref, own_ref, oth_ref, half)

    return pl.pallas_call(
        kernel,
        in_specs=[VM, VM],
        out_specs=[VM, VM],
        out_shape=[jax.ShapeDtypeStruct((half, n), f32), jax.ShapeDtypeStruct((half, n), bf16)],
        compiler_params=limit(8),
        name="decode",
    )(codes, w)


def step(attn_out, w_out, resid_in, positions, w_enc, b_enc, dec_norm, b_dec):
    y, xl, xh, z, c = (lax.axis_index(a) for a in AXES)
    x = coord("x")
    t = y * 2 + xl
    lat = xh * 8 + z * 2 + c
    own_rows = resid_in.shape[0]
    rows = attn_out.shape[0]

    def block(dy, dx, h):
        yy, xx = (y + dy) & 3, xl ^ dx
        return 8 + xx * 4 + yy if h else yy * 2 + xx

    cols = [block(dy, 1, 0) for dy in range(4)] + [block(dy, dx, 1) for dy in (2, 1, 3) for dx in (0, 1)]
    cols += [block(dy, 0, 0) for dy in range(4)] + [block(0, dx, 1) for dx in (0, 1)]

    def unit(yy, xx, h):
        return 16 + (xx & 1) * 8 + yy * 2 + (xx >> 1) if h else yy * 4 + (xx & 1) * 2 + (xx >> 1)

    four = range(4)
    units = [unit((y - s) & 3, x ^ e, 0) for s in four for e in four]
    units += [unit(y ^ e, (x - s) & 3, 1) for s in four for e in four]
    first = (y * 4 + x) * 8 + z * 2
    later = [(i + s) & 3 for i in (x, y, z) for s in four] + [(y - s) & 3 for s in four]
    y_bits = tuple((b, b ^ 1) for b in (y & 1, y >> 1))
    later += [b for pair in y_bits for b in pair] + [c, c ^ 1, xh, xh ^ 1, xl, xl ^ 1, x, y, z, first]
    homes = [((y - yy) & 3) * 2 + (xl ^ xx) for yy in four for xx in (0, 1)]
    base = lat * rows
    two_own, two_oth = c * 2, (c ^ 1) * 2
    later += homes + [base, two_own, two_oth]
    places_at = len(cols) + len(units) + 1
    placed = units[:4] + units[16:20] + units[4:16] + units[20:]
    table = lax.optimization_barrier(jnp.stack(cols + units + [t] + placed + later))
    place_at = len(cols) + len(units)
    a_send, b2, b1, b3 = project(table, 0, place_at, attn_out, w_out, resid_in, (4, 2, 2, 2), (bf16,) * 4)
    a_got = shift(a_send, "xl", 1)
    b_got = [shift(b2, "y", 2), shift(b1, "y", 1), shift(b3, "y", 3)]
    a_keep, b_keep = project(table, 10, place_at, attn_out, w_out, resid_in, (4, 2), (f32,) * 2)
    a_more = [shift((a_keep[s] + a_got[s].astype(f32)).astype(bf16), "y", s) for s in (2, 1, 3)]

    def b_part(dx):
        return b_keep[dx] + b_got[0][dx].astype(f32) + b_got[1][dx].astype(f32) + b_got[2][dx].astype(f32)

    b_more = shift(b_part(1).astype(bf16), "xl", 1)
    a_sum = a_keep[0] + a_got[0].astype(f32)
    for g in a_more:
        a_sum = a_sum + g.astype(f32)
    b_sum = b_part(0) + b_more.astype(f32)
    stream = jnp.concatenate([a_sum, b_sum], axis=1).astype(bf16)

    def template_row(r, two_core):
        xx = (r >> 3) & 3
        return (r >> 5) * 64 + (xx & 1) * 32 + (xx >> 1) * 16 + ((r >> 1) & 3) * 4 + two_core + (r & 1)

    def iota(shape, axis):
        return lax.broadcasted_iota(jnp.int32, shape, axis)

    hits = (iota((rows, 256), 0) + base == positions[None, :]).astype(bf16)

    def hot(two_core):
        rank = (template_row(iota((128, 256), 0), two_core) == iota((128, 256), 1)).astype(bf16)
        return lax.dot_general(rank, hits, (((1,), (1,)), ((), ())), preferred_element_type=f32).astype(bf16)

    def pick(h, s):
        return jnp.dot(h, s, preferred_element_type=f32).astype(bf16)

    v = pick(hot(two_own), stream) + shift(pick(hot(two_oth), stream), "c", 1)
    v = v.reshape(rows, 2, 2, 256)
    v = take(v, xh, 2) + shift(take(v, xh ^ 1, 2), "xh", 1)
    for bit in (1, 2):
        v = v + swap(v, "z", bit)
    v = v.reshape(rows, 2, 256)

    a = gather_double(v[:, 0], "x")
    b = gather_double(v[:, 1], "y")
    near = jnp.stack([a, b])
    near_oth = shift(near, "c", 1)
    acc = first_terms(table, len(cols), near, near_oth, w_enc, b_dec)
    a_far = gather_ring(a, "y")
    b_far = gather_ring(b, "x")
    a_oth = shift(a_far, "c", 1)
    b_oth = shift(b_far, "c", 1)
    s4 = stream.reshape(4, 2, own_rows, 1024)
    s_got = shift(take(s4, xl ^ 1, 1), "xl", 1)

    k = iota((256, 256), 1)
    back = (iota((256, 256), 0) == template_row(k & 127, two_own ^ ((k >> 7) * 2))).astype(bf16)
    codes, codes_out, own_a, oth_a, w_hi = autoencode(
        table, len(cols), acc, a_far, a_oth, b_far, b_oth, w_enc, b_dec, b_enc, dec_norm, back
    )
    got_a = shift(oth_a, "c", 1)
    own_b, oth_b = decode(codes, w_hi)
    got_b = shift(oth_b, "c", 1)

    h_a = (own_a + got_a.astype(f32)).astype(bf16).reshape(4, 4, 8, 4096)
    h_b = (own_b + got_b.astype(f32)).astype(bf16).reshape(4, 4, 8, 4096)
    r_a = reduce_ring(h_a, "y")
    r_b = reduce_ring(jnp.moveaxis(h_b, 1, 0), "x")
    r_a = reduce_double(r_a, "x", ((xl, xl ^ 1), (xh, xh ^ 1)))
    r_b = reduce_double(r_b, "y", y_bits)
    r = jnp.concatenate([r_a, r_b], axis=1).astype(bf16).reshape(4, 2, 8192)
    full = reduce_ring(r, "z") + b_dec

    near_s, a_s, b_s, _ = lax.optimization_barrier((near, a_far, b_far, own_b))
    s_own = take(s4, xl, 1)
    s_two = jnp.stack([s_own, s_got])
    s_rel = [shift(take(s_two, (y + s) & 3, 1), "y", s) for s in (1, 2, 3)]
    *s_rel, _ = lax.optimization_barrier((*s_rel, r))
    s_rel = [take(s_two, y, 1)] + s_rel
    s_rel = jnp.stack(s_rel).reshape(8, own_rows, 1024)

    def home(yy, xx, h):
        return take(s_rel[:, :, h * 512 : (h + 1) * 512], homes[yy * 2 + xx])

    pieces = [home(yy, xx, 0) for yy in four for xx in (0, 1)]
    pieces += [home(yy, xx, 1) for xx in (0, 1) for yy in four]
    stream_out = jnp.concatenate(pieces, axis=1)

    mine = [cut(v.reshape(-1, 128, 256), (0, first, 0), (n, 2, 256)) for v, n in ((near_s, 8), (a_s, 12), (b_s, 12))]
    mine = jnp.concatenate(mine)
    places = table[places_at : places_at + 32]
    unsort = (lax.iota(jnp.int32, 32)[:, None] == places[None, :]).astype(bf16)
    mine = jnp.dot(unsort, mine.reshape(32, 512), preferred_element_type=f32)
    mine = mine.reshape(32, 2, 256).transpose(1, 0, 2).reshape(2, 8192)
    error = jnp.mean((full - mine) ** 2, axis=1)
    return stream_out, codes_out, full.astype(bf16), error


def solution(mesh):
    fine = Mesh(mesh.devices.reshape(SIZES), AXES)
    return jax.shard_map(
        step,
        mesh=fine,
        in_specs=(
            P(LAT, TP),
            P(TP, None),
            P(LAT + TP, None),
            P(),
            P(None, TP + LAT),
            P(TP + LAT),
            P(TP + LAT),
            P(),
        ),
        out_specs=(
            P(LAT + TP, None),
            P(None, TP + LAT),
            P(TP + LAT, None),
            P(TP + LAT),
        ),
        check_vma=False,
    )
```
